512 devices in a mesh: dom: 32 (over x_hi, z), grp: 16 (over y, x_lo, core).
Axes of the slice: x: 4 (x_hi: 2, x_lo: 2; x = x_hi * 2 + x_lo), y: 4, z: 16, core: 2. Of those that a mesh axis runs over, the one named last changes fastest.
Arguments:
- adjoint_state: float32 [64, 16, 1024, 256], P('grp', None, 'dom'), may hold values from -6 to 6
- east_wind: float32 [16, 1024, 256], P(None, 'dom'), may hold values from -0.2 to 0.2
- north_wind: float32 [16, 1024, 256], P(None, 'dom'), may hold values from -0.2 to 0.2
- east_diff: float32 [16, 1024, 256], P(None, 'dom'), may hold values from 0.01 to 0.05
- north_diff: float32 [16, 1024, 256], P(None, 'dom'), may hold values from 0.01 to 0.05
- mass_flux: float32 [16, 1024, 256], P(None, 'dom'), may hold values from 0.05 to 0.45
- region_map: int32 [1024, 256], P('dom'), may hold values from 0 to 63
- cloud_top: int32 [1024, 256], P('dom'), may hold values from 1 to 15
Outputs:
- final_adjoint: float32 [64, 16, 1024, 256], P('grp', None, 'dom')
- flux_gradient: float32 [1024, 256], P('dom')
The draws below stay inside these ranges and needn't reach their ends.
Inputs may be any that keep to these rules, and one draw needn't show every extreme that they name: `region_map`: tag k of the whole set of 64 tags belongs to region k.
All inputs are finite; a program needn't handle non-finite values.
Results may differ from the reference program's by a relative error of at most 0.00002.
Values sent between devices are 32-bit elements; how exact they have to be, the bound alone decides.
A program may use at most 64 MiB of HBM per device.

```python
import math
import jax
import jax.numpy as jnp
from jax import lax

LEV = 16
NLAT = 256
ITERS = 4
NTAG = 64
NLON = 1024


def touch_ends(array, own_key, low, largest):
    index_at = [jax.random.randint(jax.random.fold_in(own_key, axis), (), 0, length) for axis, length in enumerate(array.shape)]
    main_axis = array.shape.index(max(array.shape))
    beside = index_at[:main_axis] + [(index_at[main_axis] + 1) % array.shape[main_axis]] + index_at[main_axis + 1:]
    return array.at[tuple(index_at)].set(low).at[tuple(beside)].set(largest)


def steps_of(stream_key, dims, split, least, top_value):
    factor_of = 1.0
    for dim, blocks in split:
        steps = jax.random.uniform(jax.random.fold_in(jax.random.fold_in(stream_key, 6), dim), (blocks,), jnp.float32, least / len(split), top_value / len(split))
        factor_of = factor_of * jnp.repeat(jnp.exp(steps), dims[dim] // blocks).reshape((-1,) + (1,) * (len(dims) - 1 - dim))
    return factor_of


def gaussian(own_key, dims, scale, reach, shards=(), kind=jnp.bfloat16):
    level = steps_of(own_key, dims, shards, -0.22, 0.18) if shards else 1.0
    entries = jax.random.normal(own_key, dims, jnp.float32) * scale * level
    return jnp.minimum(jnp.maximum(entries, -reach), reach).astype(kind)


def setup_inputs(seed: int = 0) -> dict:
    keys = jax.random.split(jax.random.key(seed), 9)
    return {
        "adjoint_state": gaussian(keys[0], (NTAG, LEV, NLON, NLAT), 1.0, 6.0, ((0, 16), (2, 32)), jnp.float32),
        "east_wind": jnp.clip(jax.random.uniform(keys[1], (LEV, NLON, NLAT), jnp.float32, -0.2, 0.2) * steps_of(keys[1], (LEV, NLON, NLAT), ((1, 32),), -0.4, 0.0), -0.2, 0.2),
        "north_wind": jnp.clip(jax.random.uniform(keys[2], (LEV, NLON, NLAT), jnp.float32, -0.2, 0.2) * steps_of(keys[2], (LEV, NLON, NLAT), ((1, 32),), -0.4, 0.0), -0.2, 0.2),
        "east_diff": jnp.clip(jnp.exp(math.log(0.05) - 1.609438 * jax.random.uniform(keys[3], (LEV, NLON, NLAT), jnp.float32) ** steps_of(keys[3], (LEV, NLON, NLAT), ((1, 32),), -0.2, 0.2)), 0.01, 0.05),
        "north_diff": jnp.clip(jnp.exp(math.log(0.05) - 1.609438 * jax.random.uniform(keys[4], (LEV, NLON, NLAT), jnp.float32) ** steps_of(keys[4], (LEV, NLON, NLAT), ((1, 32),), -0.2, 0.2)), 0.01, 0.05),
        "mass_flux": jnp.clip(0.05 + 0.39999999 * jax.random.uniform(keys[5], (LEV, NLON, NLAT), jnp.float32) ** steps_of(keys[5], (LEV, NLON, NLAT), ((1, 32),), -0.2, 0.2), 0.05, 0.45),
        "region_map": touch_ends(jax.random.randint(keys[6], (NLON, NLAT), 0, NTAG), jax.random.fold_in(keys[6], 1), 0, NTAG - 1).astype(jnp.int32),
        "cloud_top": touch_ends(jax.random.randint(keys[7], (NLON, NLAT), 1, LEV), jax.random.fold_in(keys[7], 1), 1, LEV - 1).astype(jnp.int32),
    }


def reference(adjoint_state, east_wind, north_wind, east_diff, north_diff, mass_flux, region_map, cloud_top):
    east_coef = jnp.maximum(east_wind, 0.0) + east_diff
    west_prime = jnp.maximum(-east_wind, 0.0) + east_diff
    west_coef = jnp.roll(west_prime, 1, axis=1)
    row_ids = lax.broadcasted_iota(jnp.int32, east_wind.shape, 2)
    north_coef = (jnp.maximum(north_wind, 0.0) + north_diff) * (row_ids < NLAT - 1).astype(jnp.float32)
    south_prime = jnp.maximum(-north_wind, 0.0) + north_diff
    south_coef = jnp.concatenate([jnp.zeros_like(south_prime[..., :1]), south_prime[..., :-1]], axis=-1)
    level_ids = lax.broadcasted_iota(jnp.int32, mass_flux.shape, 0)
    updraft = mass_flux * (level_ids < cloud_top[None]).astype(jnp.float32)
    lam = adjoint_state
    accum = jnp.zeros((NTAG, NLON, NLAT), jnp.float32)
    for step in range(ITERS):
        east = jnp.roll(lam, -1, axis=2)
        west = jnp.roll(lam, 1, axis=2)
        north = jnp.concatenate([lam[..., 1:], lam[..., -1:]], axis=-1)
        south = jnp.concatenate([lam[..., :1], lam[..., :-1]], axis=-1)
        h = lam + east_coef * (east - lam) + west_coef * (west - lam) + north_coef * (north - lam) + south_coef * (south - lam)
        above = jnp.concatenate([h[:, 1:], h[:, -1:]], axis=1)
        lam = h + updraft * (above - h)
        accum = accum + lam[:, 0]
    tag_ids = lax.broadcasted_iota(jnp.int32, (NTAG, NLON, NLAT), 0)
    select = (region_map[None] == tag_ids).astype(jnp.float32)
    flux_gradient = jnp.sum(select * accum, axis=0)
    return lam, flux_gradient
```

```python
import jax
import jax.numpy as jnp
from jax import lax
from jax.experimental import pallas as pl
from jax.experimental.pallas import tpu as pltpu
from jax.sharding import PartitionSpec as P

ITERS = 4
MESH = pl.DeviceIdType.MESH
CE, CW, CN, CS, C0, UP = range(6)


def turned(value):
    return jnp.swapaxes(value, 0, 1)


def kernel(
    x_ref, ew_ref, nw_ref, ed_ref, nd_ref, mf_ref, reg_ref, top_ref,
    lam_ref, grad_ref,
    raw, wraw, state, coef, ctop, regs, halo, whalo, thalo, save_l, save_r, west_end,
    acc, part1, part2, got1, got2,
    in_sem, xs_sem, xr_sem, ws_sem, wr_sem, fs_sem, fr_sem, g1s, g1r, g2s, g2r,
):
    tags, levels, cols, lats = x_ref.shape
    groups = lax.axis_size("grp")
    count = lax.axis_size("dom")
    me = lax.axis_index("dom")
    grp = lax.axis_index("grp")
    east_dev = lax.rem(me + 1, count)
    west_dev = lax.rem(me + count - 1, count)
    half = lax.rem(grp, 2)
    twin = grp + 1 - 2 * half
    H = ITERS
    hl = levels // 2

    winds = (ew_ref, ed_ref, nw_ref, nd_ref, mf_ref)
    barrier = pltpu.get_barrier_semaphore()
    for q in (east_dev, west_dev):
        pl.semaphore_signal(barrier, inc=1, device_id={"dom": q}, device_id_type=MESH)
    for d in range(1, groups):
        pl.semaphore_signal(
            barrier, inc=1, device_id={"grp": lax.rem(grp + d, groups)}, device_id_type=MESH
        )
    loads = [pltpu.make_async_copy(w, wraw.at[a], in_sem.at[a]) for a, w in enumerate(winds)]
    loads.append(pltpu.make_async_copy(top_ref, ctop, in_sem.at[5]))
    loads.append(pltpu.make_async_copy(reg_ref, regs, in_sem.at[6]))
    loads.append(pltpu.make_async_copy(x_ref, raw, in_sem.at[7]))
    for c in loads:
        c.start()

    lane = lax.broadcasted_iota(jnp.int32, (8, levels, lats), 2)
    level = lax.broadcasted_iota(jnp.int32, (levels, 8, lats), 0)

    def derive(ew, ed, nw, nd, mf, top, before):
        lift = mf * (level < jnp.minimum(top, levels - 1)[None]).astype(jnp.float32)
        ew, ed, nw, nd, lift = turned(ew), turned(ed), turned(nw), turned(nd), turned(lift)
        east = jnp.maximum(ew, 0.0) + ed
        prime = jnp.maximum(-ew, 0.0) + ed
        west = jnp.concatenate([before[None], prime[:-1]], axis=0)
        north = jnp.where(lane < lats - 1, jnp.maximum(nw, 0.0) + nd, 0.0)
        south = jnp.where(lane > 0, pltpu.roll(jnp.maximum(-nw, 0.0) + nd, 1, 2), 0.0)
        keep = 1.0 - east - west - north - south
        return (east, west, north, south, keep, lift), prime

    for c in loads[:6]:
        c.wait()

    def derive_tile(i, before):
        at = pl.ds(pl.multiple_of(8 * i, 8), 8)
        made, prime = derive(*[wraw[a, :, at, :] for a in range(5)], ctop[at, :], before)
        for m in range(6):
            coef[m, pl.ds(H + 8 * i, 8)] = made[m]
        return prime[7]

    west_end[...] = lax.fori_loop(
        0, cols // 8, derive_tile, jnp.zeros((levels, lats), jnp.float32)
    )

    loads[7].wait()
    loads[6].wait()

    @pl.loop(0, tags)
    def _(k):
        for i in range(cols // 8):
            state[k, pl.ds(H + 8 * i, 8)] = turned(raw[k, :, 8 * i : 8 * i + 8, :])

    pl.semaphore_wait(barrier, groups + 1)

    mine = pl.ds(pl.multiple_of(half * hl, hl), hl)
    sends = []
    sides = ((0, east_dev, cols - H, 0), (1, west_dev, 0, H))
    for s, q, src, dst in sides:
        for a, w in enumerate(winds):
            sends.append(
                pltpu.make_async_remote_copy(
                    w.at[mine, src : src + H, :],
                    whalo.at[a, mine, dst : dst + H, :],
                    ws_sem.at[s, a], wr_sem.at[s, a],
                    device_id={"dom": q}, device_id_type=MESH,
                )
            )
        sends.append(
            pltpu.make_async_remote_copy(
                top_ref.at[src : src + H, :], thalo.at[dst : dst + H, :],
                ws_sem.at[s, 5], wr_sem.at[s, 5],
                device_id={"dom": q}, device_id_type=MESH,
            )
        )
    for c in sends:
        c.start()
    xsends = []
    for p in range(tags // 2):
        for s, q, src, dst in sides:
            c = pltpu.make_async_remote_copy(
                x_ref.at[2 * p : 2 * p + 2, :, src : src + H, :],
                halo.at[2 * p : 2 * p + 2, :, dst : dst + H, :],
                xs_sem.at[s, p], xr_sem.at[s, p],
                device_id={"dom": q}, device_id_type=MESH,
            )
            c.start()
            xsends.append(c)

    def advance(left, cen, right, c):
        north = pltpu.roll(cen, lats - 1, 2)
        south = pltpu.roll(cen, 1, 2)
        h = (
            coef[C0, c][None] * cen
            + coef[CE, c][None] * right
            + coef[CW, c][None] * left
            + coef[CN, c][None] * north
            + coef[CS, c][None] * south
        )
        above = pltpu.roll(h, levels - 1, 1)
        return h + coef[UP, c][None] * (above - h)

    acc[...] = jnp.zeros_like(acc)

    @pl.loop(0, tags // 2)
    def _(p):
        ks = pl.ds(2 * p, 2)

        @pl.loop(1, ITERS + 1)
        def _(t):
            left = state[ks, H + t - 1]
            cen = state[ks, H + t]
            save_l[ks, t - 1] = cen

            def body(c, carry):
                left, cen = carry
                right = state[ks, c + 1]
                new = advance(left, cen, right, c)
                state[ks, c] = new
                acc[ks, c] += new[:, 0:8]
                return cen, right

            left, cen = lax.fori_loop(H + t, H + cols - t, body, (left, cen))
            save_r[ks, t - 1] = left

    tag0 = grp * tags
    row = lax.broadcasted_iota(jnp.int32, (8, lats), 0)

    for i in range(cols // 8):
        here = regs[8 * i : 8 * i + 8, :]
        total = jnp.zeros((8, lats), jnp.float32)
        for k in range(tags):
            top = turned(acc[k, H + 8 * i : H + 8 * i + 8])[0]
            total += jnp.where(here == tag0 + k, top, 0.0)
        part1[8 * i : 8 * i + 8, :] = total

    def spread(part, got, ss, rs):
        out = []
        for d in range(1, groups):
            c = pltpu.make_async_remote_copy(
                part, got.at[d - 1], ss.at[d - 1], rs.at[d - 1],
                device_id={"grp": lax.rem(grp + d, groups)}, device_id_type=MESH,
            )
            c.start()
            out.append(c)
        return out

    early = spread(part1, got1, g1s, g1r)

    @pl.loop(0, tags)
    def _(k):
        for s in (0, H + cols - 4):
            acc[k, s : s + 8] = jnp.zeros((8, 8, lats), jnp.float32)
        for i in range(1, cols // 8 - 1):
            lam_ref[k, :, 8 * i : 8 * i + 8, :] = turned(state[k, H + 8 * i : H + 8 * i + 8])

    for c in sends:
        c.wait_recv()
    share = pltpu.make_async_remote_copy(
        whalo.at[:, mine], whalo.at[:, mine], fs_sem, fr_sem,
        device_id={"grp": twin}, device_id_type=MESH,
    )
    share.start()
    share.wait_recv()

    made, prime = derive(*[whalo[a] for a in range(5)], thalo[...], jnp.zeros((levels, lats), jnp.float32))
    for m in range(6):
        coef[m, 0:H] = made[m][0:H]
        coef[m, H + cols : 2 * H + cols] = made[m][H:]
    first = prime[H - 1]
    coef[CW, H] = first
    coef[C0, H] = coef[C0, H] - first
    last = west_end[...]
    coef[CW, H + cols] = last
    coef[C0, H + cols] = made[C0][H] + made[CW][H] - last

    for p in range(tags // 2):
        for c in xsends[2 * p : 2 * p + 2]:
            c.wait_recv()
        for k in (2 * p, 2 * p + 1):
            edge = turned(halo[k])
            state[k, 0:H] = edge[0:H]
            state[k, H + cols : 2 * H + cols] = edge[H:]
        ks = pl.ds(2 * p, 2)

        @pl.loop(1, ITERS + 1)
        def _(t):
            left, cen = state[ks, t - 1], state[ks, t]
            for n in range(H):
                right = state[ks, t + n + 1] if n < H - 1 else save_l[ks, t - 1]
                new = advance(left, cen, right, t + n)
                state[ks, t + n] = new
                acc[ks, t + n] += new[:, 0:8]
                left, cen = cen, right
            base = H + cols - t
            left, cen = save_r[ks, t - 1], state[ks, base]
            for n in range(H):
                right = state[ks, base + n + 1]
                new = advance(left, cen, right, base + n)
                state[ks, base + n] = new
                acc[ks, base + n] += new[:, 0:8]
                left, cen = cen, right

    here = jnp.where(row < H, regs[0:8, :], regs[cols - 8 : cols, :])
    total = jnp.zeros((8, lats), jnp.float32)
    for k in range(tags):
        ends = jnp.concatenate([acc[k, H : 2 * H], acc[k, cols : cols + H]], axis=0)
        total += jnp.where(here == tag0 + k, turned(ends)[0], 0.0)
    part2[...] = total
    late = spread(part2, got2, g2s, g2r)

    @pl.loop(0, tags)
    def _(k):
        for i in (0, cols // 8 - 1):
            lam_ref[k, :, 8 * i : 8 * i + 8, :] = turned(state[k, H + 8 * i : H + 8 * i + 8])

    for c in early:
        c.wait_recv()
    grad_ref[...] = lax.fori_loop(
        0, groups - 1, lambda d, v: v + got1[d], part1[...]
    )
    for c in late:
        c.wait_recv()
    ends = lax.fori_loop(0, groups - 1, lambda d, v: v + got2[d], part2[...])
    grad_ref[0:8, :] += jnp.where(row < H, ends, 0.0)
    grad_ref[cols - 8 : cols, :] += jnp.where(row >= H, ends, 0.0)

    for c in sends + xsends + [share] + early + late:
        c.wait_send()


def local(
    adjoint_state, east_wind, north_wind, east_diff, north_diff, mass_flux, region_map, cloud_top
):
    tags, levels, cols, lats = adjoint_state.shape
    groups = lax.axis_size("grp")
    f32 = jnp.float32
    wide = cols + 2 * ITERS
    dma = pltpu.SemaphoreType.DMA
    scratch = [
        pltpu.VMEM((tags, levels, cols, lats), f32),
        pltpu.VMEM((5, levels, cols, lats), f32),
        pltpu.VMEM((tags, wide, levels, lats), f32),
        pltpu.VMEM((6, wide, levels, lats), f32),
        pltpu.VMEM((cols, lats), jnp.int32),
        pltpu.VMEM((cols, lats), jnp.int32),
        pltpu.VMEM((tags, levels, 2 * ITERS, lats), f32),
        pltpu.VMEM((5, levels, 2 * ITERS, lats), f32),
        pltpu.VMEM((2 * ITERS, lats), jnp.int32),
        pltpu.VMEM((tags, ITERS, levels, lats), f32),
        pltpu.VMEM((tags, ITERS, levels, lats), f32),
        pltpu.VMEM((levels, lats), f32),
        pltpu.VMEM((tags, wide, 8, lats), f32),
        pltpu.VMEM((cols, lats), f32),
        pltpu.VMEM((2 * ITERS, lats), f32),
        pltpu.VMEM((groups - 1, cols, lats), f32),
        pltpu.VMEM((groups - 1, 2 * ITERS, lats), f32),
        dma((8,)),
        dma((2, tags // 2)),
        dma((2, tags // 2)),
        dma((2, 6)),
        dma((2, 6)),
        dma,
        dma,
        dma((groups - 1,)),
        dma((groups - 1,)),
        dma((groups - 1,)),
        dma((groups - 1,)),
    ]
    return pl.pallas_call(
        kernel,
        name="adjoint_transport",
        out_shape=(
            pltpu.VMEM((tags, levels, cols, lats), f32),
            pltpu.VMEM((cols, lats), f32),
        ),
        in_specs=[pl.BlockSpec(memory_space=pltpu.HBM)] * 8,
        out_specs=(
            pl.BlockSpec(memory_space=pltpu.VMEM),
            pl.BlockSpec(memory_space=pltpu.VMEM),
        ),
        scratch_shapes=scratch,
        compiler_params=pltpu.CompilerParams(
            collective_id=0, has_side_effects=True, vmem_limit_bytes=58 << 20
        ),
    )(
        adjoint_state, east_wind, north_wind, east_diff, north_diff, mass_flux, region_map,
        cloud_top,
    )


def solution(mesh):
    return jax.shard_map(
        local,
        mesh=mesh,
        in_specs=(
            P("grp", None, "dom", None),
            P(None, "dom", None),
            P(None, "dom", None),
            P(None, "dom", None),
            P(None, "dom", None),
            P(None, "dom", None),
            P("dom", None),
            P("dom", None),
        ),
        out_specs=(P("grp", None, "dom", None), P("dom", None)),
        check_vma=False,
    )
```

```python
import jax
import jax.numpy as jnp
from jax import lax
from jax.experimental import pallas as pl
from jax.experimental.pallas import tpu as pltpu
from jax.sharding import PartitionSpec as P

ITERS = 4
MESH = pl.DeviceIdType.MESH
CE, CW, CN, CS, C0, UP = range(6)


def turned(value):
    return jnp.swapaxes(value, 0, 1)


def kernel(
    x_ref, ew_ref, nw_ref, ed_ref, nd_ref, mf_ref, reg_ref, top_ref,
    lam_ref, grad_ref,
    raw, wraw, state, coef, ctop, regs, halo, whalo, thalo, save_l, save_r, west_end,
    acc, part1, part2, got1, got2, surf, keep_first,
    in_sem, xs_sem, xr_sem, ws_sem, wr_sem, ts_sem, tr_sem, fs_sem, fr_sem, g1s, g1r, g2s, g2r,
):
    tags, levels, cols, lats = x_ref.shape
    groups = lax.axis_size("grp")
    count = lax.axis_size("dom")
    me = lax.axis_index("dom")
    grp = lax.axis_index("grp")
    east_dev = lax.rem(me + 1, count)
    west_dev = lax.rem(me + count - 1, count)
    half = lax.rem(grp, 2)
    twin = grp + 1 - 2 * half
    H = ITERS
    low = ITERS + 2

    winds = (ew_ref, ed_ref, nw_ref, nd_ref, mf_ref)
    barrier = pltpu.get_barrier_semaphore()
    for q in (east_dev, west_dev):
        pl.semaphore_signal(barrier, inc=1, device_id={"dom": q}, device_id_type=MESH)
    for d in range(1, groups):
        pl.semaphore_signal(
            barrier, inc=1, device_id={"grp": lax.rem(grp + d, groups)}, device_id_type=MESH
        )
    loads = [pltpu.make_async_copy(w, wraw.at[a], in_sem.at[a]) for a, w in enumerate(winds)]
    loads.append(pltpu.make_async_copy(top_ref, ctop, in_sem.at[5]))
    loads.append(pltpu.make_async_copy(reg_ref, regs, in_sem.at[6]))
    loads.append(pltpu.make_async_copy(x_ref, raw, in_sem.at[7]))
    for c in loads:
        c.start()

    pl.semaphore_wait(barrier, groups + 1)

    sides = ((0, east_dev, cols - H, 0), (1, west_dev, 0, H))
    spans = ((0, low // 2), (low, (levels - low) // 2))
    mine = [pl.ds(lo + half * n, n) for lo, n in spans]

    def wind_sends(part):
        out = []
        for s, q, src, dst in sides:
            for a, w in enumerate(winds):
                out.append(
                    pltpu.make_async_remote_copy(
                        w.at[mine[part], src : src + H, :],
                        whalo.at[a, mine[part], dst : dst + H, :],
                        ws_sem.at[part, s, a], wr_sem.at[part, s, a],
                        device_id={"dom": q}, device_id_type=MESH,
                    )
                )
        for c in out:
            c.start()
        return out

    def state_sends(at, tag, lev):
        out = []
        for s, q, src, dst in sides:
            out.append(
                pltpu.make_async_remote_copy(
                    x_ref.at[tag, lev, src : src + H, :],
                    halo.at[tag, lev, dst : dst + H, :],
                    xs_sem.at[at, s], xr_sem.at[at, s],
                    device_id={"dom": q}, device_id_type=MESH,
                )
            )
        for c in out:
            c.start()
        return out

    low_winds = wind_sends(0)
    tops = []
    for s, q, src, dst in sides:
        c = pltpu.make_async_remote_copy(
            top_ref.at[src : src + H, :], thalo.at[dst : dst + H, :],
            ts_sem.at[s], tr_sem.at[s],
            device_id={"dom": q}, device_id_type=MESH,
        )
        c.start()
        tops.append(c)
    low_state = state_sends(0, slice(0, tags), slice(0, low))
    high_winds = wind_sends(1)
    high_state = [
        state_sends(1 + p, slice(2 * p, 2 * p + 2), slice(low, levels)) for p in range(tags // 2)
    ]

    def share_part(part):
        return pltpu.make_async_remote_copy(
            whalo.at[:, mine[part]], whalo.at[:, mine[part]], fs_sem.at[part], fr_sem.at[part],
            device_id={"grp": twin}, device_id_type=MESH,
        )

    def derive(ew, ed, nw, nd, mf, top, before):
        level = lax.broadcasted_iota(jnp.int32, ew.shape, 0)
        lane = lax.broadcasted_iota(jnp.int32, (8, ew.shape[0], lats), 2)
        lift = mf * (level < jnp.minimum(top, levels - 1)[None]).astype(jnp.float32)
        ew, ed, nw, nd, lift = turned(ew), turned(ed), turned(nw), turned(nd), turned(lift)
        east = jnp.maximum(ew, 0.0) + ed
        prime = jnp.maximum(-ew, 0.0) + ed
        west = jnp.concatenate([before[None], prime[:-1]], axis=0)
        north = jnp.where(lane < lats - 1, jnp.maximum(nw, 0.0) + nd, 0.0)
        south = jnp.where(lane > 0, pltpu.roll(jnp.maximum(-nw, 0.0) + nd, 1, 2), 0.0)
        keep = 1.0 - east - west - north - south
        return (east, west, north, south, keep, lift), prime

    for c in loads[:6]:
        c.wait()

    def derive_tile(i, before):
        at = pl.ds(pl.multiple_of(8 * i, 8), 8)
        made, prime = derive(*[wraw[a, :, at, :] for a in range(5)], ctop[at, :], before)
        for m in range(6):
            coef[m, pl.ds(H + 8 * i, 8)] = made[m]
        return prime[7]

    west_end[...] = lax.fori_loop(
        0, cols // 8, derive_tile, jnp.zeros((levels, lats), jnp.float32)
    )

    keep_first[...] = coef[C0, H]
    loads[7].wait()
    loads[6].wait()

    @pl.loop(0, tags)
    def _(k):
        for i in range(cols // 8):
            state[k, pl.ds(H + 8 * i, 8)] = turned(raw[k, :, 8 * i : 8 * i + 8, :])

    def advance(left, cen, right, c):
        lv = pl.ds(0, cen.shape[1])
        north = pltpu.roll(cen, lats - 1, 2)
        south = pltpu.roll(cen, 1, 2)
        h = (
            coef[C0, c, lv][None] * cen
            + coef[CE, c, lv][None] * right
            + coef[CW, c, lv][None] * left
            + coef[CN, c, lv][None] * north
            + coef[CS, c, lv][None] * south
        )
        above = pltpu.roll(h, cen.shape[1] - 1, 1)
        return h + coef[UP, c, lv][None] * (above - h)

    acc[...] = jnp.zeros_like(acc)

    @pl.loop(0, tags // 2)
    def _(p):
        ks = pl.ds(2 * p, 2)

        def run(c, carry, n):
            old = list(carry) + [state[ks, c + 1 + j] for j in range(n)]
            for j in range(n):
                new = advance(old[j], old[j + 1], old[j + 2], c + j)
                state[ks, c + j] = new
                acc[ks, c + j] += new[:, 0:8]
            return old[n], old[n + 1]

        for t in range(1, ITERS + 1):
            start, size = H + t, cols - 2 * t
            carry = state[ks, start - 1], state[ks, start]
            save_l[ks, t - 1] = carry[1]
            if size % 4:
                carry = run(start, carry, size % 4)
                start += size % 4
            carry = lax.fori_loop(
                0, size // 4, lambda b, v: run(start + 4 * b, v, 4), carry
            )
            save_r[ks, t - 1] = carry[0]

    tag0 = grp * tags
    row = lax.broadcasted_iota(jnp.int32, (8, lats), 0)

    for i in range(cols // 8):
        here = regs[8 * i : 8 * i + 8, :]
        total = jnp.zeros((8, lats), jnp.float32)
        for k in range(tags):
            top = turned(acc[k, H + 8 * i : H + 8 * i + 8])[0]
            total += jnp.where(here == tag0 + k, top, 0.0)
        part1[8 * i : 8 * i + 8, :] = total

    def spread(part, got, ss, rs):
        out = []
        for d in range(1, groups):
            c = pltpu.make_async_remote_copy(
                part, got.at[d - 1], ss.at[d - 1], rs.at[d - 1],
                device_id={"grp": lax.rem(grp + d, groups)}, device_id_type=MESH,
            )
            c.start()
            out.append(c)
        return out

    early = spread(part1, got1, g1s, g1r)

    @pl.loop(0, tags)
    def _(k):
        for s in (0, H + cols - 4):
            acc[k, s : s + 8] = jnp.zeros((8, 8, lats), jnp.float32)
        for i in range(1, cols // 8 - 1):
            lam_ref[k, :, 8 * i : 8 * i + 8, :] = turned(state[k, H + 8 * i : H + 8 * i + 8])

    def edge_coefs(lv, size):
        pad = levels // 2 * (size < levels)

        def part(a):
            if not pad:
                return whalo[a]
            return jnp.concatenate(
                [whalo[a, 0:size], jnp.zeros((pad - size, 2 * H, lats), jnp.float32)], axis=0
            )

        made, prime = derive(
            *[part(a) for a in range(5)], thalo[...], jnp.zeros((lv.size, lats), jnp.float32)
        )
        for m in range(6):
            coef[m, 0:H, lv] = made[m][0:H]
            coef[m, H + cols : 2 * H + cols, lv] = made[m][H:]
        first = prime[H - 1]
        coef[CW, H, lv] = first
        coef[C0, H, lv] = keep_first[lv] - first
        last = west_end[lv]
        coef[CW, H + cols, lv] = last
        coef[C0, H + cols, lv] = made[C0][H] + made[CW][H] - last

    def edges(store, ks, lv, shift, count_in):
        @pl.loop(1, ITERS + 1)
        def _(t):
            for base, at in ((t, t), (H + cols - t, H + cols - t - shift)):
                if base is t:
                    old = [store[ks, at - 1 + n] for n in range(H + 1)]
                    old.append(save_l[ks, t - 1, lv])
                else:
                    old = [save_r[ks, t - 1, lv]]
                    old += [store[ks, at + n] for n in range(H + 1)]
                for n in range(H):
                    new = advance(old[n], old[n + 1], old[n + 2], base + n)
                    store[ks, at + n] = new
                    if count_in:
                        acc[ks, base + n] += new

    for c in low_winds:
        c.wait_recv()
    share0 = share_part(0)
    share0.start()
    for c in tops + low_state:
        c.wait_recv()
    share0.wait_recv()
    edge_coefs(pl.ds(0, 8), low)

    @pl.loop(0, tags // 2)
    def _(p):
        for j in range(2):
            k = 2 * p + j
            ring = turned(
                jnp.concatenate(
                    [halo[k, 0:low], jnp.zeros((8 - low, 2 * H, lats), jnp.float32)], axis=0
                )
            )
            surf[k, 0:H] = ring[0:H]
            surf[k, 3 * H : 4 * H] = ring[H:]
            surf[k, H : 2 * H] = state[k, H : 2 * H, 0:8]
            surf[k, 2 * H : 3 * H] = state[k, cols : cols + H, 0:8]
        edges(surf, pl.ds(2 * p, 2), pl.ds(0, 8), cols - 2 * H, True)

    here = jnp.where(row < H, regs[0:8, :], regs[cols - 8 : cols, :])
    total = jnp.zeros((8, lats), jnp.float32)
    for k in range(tags):
        ends = jnp.concatenate([acc[k, H : 2 * H], acc[k, cols : cols + H]], axis=0)
        total += jnp.where(here == tag0 + k, turned(ends)[0], 0.0)
    part2[...] = total
    late = spread(part2, got2, g2s, g2r)

    for c in high_winds:
        c.wait_recv()
    share1 = share_part(1)
    share1.start()
    share1.wait_recv()
    edge_coefs(pl.ds(0, levels), levels)

    for p in range(tags // 2):
        for c in high_state[p]:
            c.wait_recv()
        for k in (2 * p, 2 * p + 1):
            ring = turned(halo[k])
            state[k, 0:H] = ring[0:H]
            state[k, H + cols : 2 * H + cols] = ring[H:]
        edges(state, pl.ds(2 * p, 2), pl.ds(0, levels), 0, False)
        for k in (2 * p, 2 * p + 1):
            for i in (0, cols // 8 - 1):
                lam_ref[k, :, 8 * i : 8 * i + 8, :] = turned(state[k, H + 8 * i : H + 8 * i + 8])

    for c in early:
        c.wait_recv()
    grad_ref[...] = lax.fori_loop(
        0, groups - 1, lambda d, v: v + got1[d], part1[...]
    )
    for c in late:
        c.wait_recv()
    ends = lax.fori_loop(0, groups - 1, lambda d, v: v + got2[d], part2[...])
    grad_ref[0:8, :] += jnp.where(row < H, ends, 0.0)
    grad_ref[cols - 8 : cols, :] += jnp.where(row >= H, ends, 0.0)

    sent = low_winds + tops + low_state + high_winds + high_state[0] + high_state[1]
    for c in sent + [share0, share1] + early + late:
        c.wait_send()


def local(
    adjoint_state, east_wind, north_wind, east_diff, north_diff, mass_flux, region_map, cloud_top
):
    tags, levels, cols, lats = adjoint_state.shape
    groups = lax.axis_size("grp")
    f32 = jnp.float32
    wide = cols + 2 * ITERS
    dma = pltpu.SemaphoreType.DMA
    scratch = [
        pltpu.VMEM((tags, levels, cols, lats), f32),
        pltpu.VMEM((5, levels, cols, lats), f32),
        pltpu.VMEM((tags, wide, levels, lats), f32),
        pltpu.VMEM((6, wide, levels, lats), f32),
        pltpu.VMEM((cols, lats), jnp.int32),
        pltpu.VMEM((cols, lats), jnp.int32),
        pltpu.VMEM((tags, levels, 2 * ITERS, lats), f32),
        pltpu.VMEM((5, levels, 2 * ITERS, lats), f32),
        pltpu.VMEM((2 * ITERS, lats), jnp.int32),
        pltpu.VMEM((tags, ITERS, levels, lats), f32),
        pltpu.VMEM((tags, ITERS, levels, lats), f32),
        pltpu.VMEM((levels, lats), f32),
        pltpu.VMEM((tags, wide, 8, lats), f32),
        pltpu.VMEM((cols, lats), f32),
        pltpu.VMEM((2 * ITERS, lats), f32),
        pltpu.VMEM((groups - 1, cols, lats), f32),
        pltpu.VMEM((groups - 1, 2 * ITERS, lats), f32),
        pltpu.VMEM((tags, 4 * ITERS, 8, lats), f32),
        pltpu.VMEM((levels, lats), f32),
        dma((8,)),
        dma((1 + tags // 2, 2)),
        dma((1 + tags // 2, 2)),
        dma((2, 2, 5)),
        dma((2, 2, 5)),
        dma((2,)),
        dma((2,)),
        dma((2,)),
        dma((2,)),
        dma((groups - 1,)),
        dma((groups - 1,)),
        dma((groups - 1,)),
        dma((groups - 1,)),
    ]
    return pl.pallas_call(
        kernel,
        name="adjoint_transport",
        out_shape=(
            pltpu.VMEM((tags, levels, cols, lats), f32),
            pltpu.VMEM((cols, lats), f32),
        ),
        in_specs=[pl.BlockSpec(memory_space=pltpu.HBM)] * 8,
        out_specs=(
            pl.BlockSpec(memory_space=pltpu.VMEM),
            pl.BlockSpec(memory_space=pltpu.VMEM),
        ),
        scratch_shapes=scratch,
        compiler_params=pltpu.CompilerParams(
            collective_id=0, has_side_effects=True, vmem_limit_bytes=58 << 20
        ),
    )(
        adjoint_state, east_wind, north_wind, east_diff, north_diff, mass_flux, region_map,
        cloud_top,
    )


def solution(mesh):
    return jax.shard_map(
        local,
        mesh=mesh,
        in_specs=(
            P("grp", None, "dom", None),
            P(None, "dom", None),
            P(None, "dom", None),
            P(None, "dom", None),
            P(None, "dom", None),
            P(None, "dom", None),
            P("dom", None),
            P("dom", None),
        ),
        out_specs=(P("grp", None, "dom", None), P("dom", None)),
        check_vma=False,
    )
```

```python
import jax
import jax.numpy as jnp
from jax import lax
from jax.experimental import pallas as pl
from jax.experimental.pallas import tpu as pltpu
from jax.sharding import PartitionSpec as P

ITERS = 4
MESH = pl.DeviceIdType.MESH
CE, CW, CN, CS, C0, UP = range(6)


def turned(value):
    return jnp.swapaxes(value, 0, 1)


def kernel(
    x_ref, ew_ref, nw_ref, ed_ref, nd_ref, mf_ref, reg_ref, top_ref,
    lam_ref, grad_ref,
    raw, wraw, state, coef, ctop, regs, halo, whalo, thalo, save_l, save_r, west_end,
    acc, edge_acc, part1, part2, near1, near2, mid1, mid2, far1, far2, surf, keep_first,
    in_sem, xs_sem, xr_sem, ws_sem, wr_sem, ts_sem, tr_sem, fs_sem, fr_sem, n1_sem, n2_sem, f1_sem, f2_sem,
):
    tags, levels, cols, lats = x_ref.shape
    groups = lax.axis_size("grp")
    count = lax.axis_size("dom")
    me = lax.axis_index("dom")
    grp = lax.axis_index("grp")
    east_dev = lax.rem(me + 1, count)
    west_dev = lax.rem(me + count - 1, count)
    half = lax.rem(grp, 2)
    twin = grp + 1 - 2 * half
    lane4 = lax.rem(grp, 4)
    near = [grp - lane4 + lax.rem(lane4 + d, 4) for d in range(1, 4)]
    far = [lax.rem(grp + 4 * d, groups) for d in range(1, groups // 4)]
    H = ITERS
    low = ITERS + 2

    winds = (ew_ref, ed_ref, nw_ref, nd_ref, mf_ref)
    barrier = pltpu.get_barrier_semaphore()
    for q in (east_dev, west_dev):
        pl.semaphore_signal(barrier, inc=1, device_id={"dom": q}, device_id_type=MESH)
    for q in near + far:
        pl.semaphore_signal(barrier, inc=1, device_id={"grp": q}, device_id_type=MESH)
    loads = [pltpu.make_async_copy(w, wraw.at[a], in_sem.at[a]) for a, w in enumerate(winds)]
    loads.append(pltpu.make_async_copy(top_ref, ctop, in_sem.at[5]))
    loads.append(pltpu.make_async_copy(reg_ref, regs, in_sem.at[6]))
    loads.append(pltpu.make_async_copy(x_ref, raw, in_sem.at[7]))
    for c in loads:
        c.start()

    def derive(ew, ed, nw, nd, mf, top, before):
        level = lax.broadcasted_iota(jnp.int32, ew.shape, 0)
        lane = lax.broadcasted_iota(jnp.int32, (8, ew.shape[0], lats), 2)
        lift = mf * (level < jnp.minimum(top, levels - 1)[None]).astype(jnp.float32)
        ew, ed, nw, nd, lift = turned(ew), turned(ed), turned(nw), turned(nd), turned(lift)
        east = jnp.maximum(ew, 0.0) + ed
        prime = jnp.maximum(-ew, 0.0) + ed
        west = jnp.concatenate([before[None], prime[:-1]], axis=0)
        north = jnp.where(lane < lats - 1, jnp.maximum(nw, 0.0) + nd, 0.0)
        south = jnp.where(lane > 0, pltpu.roll(jnp.maximum(-nw, 0.0) + nd, 1, 2), 0.0)
        keep = 1.0 - east - west - north - south
        return (east, west, north, south, keep, lift), prime

    for c in loads[:6]:
        c.wait()

    def derive_tile(i, before):
        at = pl.ds(pl.multiple_of(8 * i, 8), 8)
        made, prime = derive(*[wraw[a, :, at, :] for a in range(5)], ctop[at, :], before)
        for m in range(6):
            coef[m, pl.ds(H + 8 * i, 8)] = made[m]
        return prime[7]

    west_end[...] = lax.fori_loop(
        0, cols // 8, derive_tile, jnp.zeros((levels, lats), jnp.float32)
    )

    keep_first[...] = coef[C0, H]
    loads[7].wait()
    loads[6].wait()

    @pl.loop(0, tags)
    def _(k):
        @pl.loop(0, cols // 8)
        def _(i):
            at = pl.multiple_of(8 * i, 8)
            state[k, pl.ds(H + 8 * i, 8)] = turned(raw[k, :, pl.ds(at, 8), :])

    pl.semaphore_wait(barrier, 2 + len(near) + len(far))

    sides = ((0, east_dev, cols - H, 0), (1, west_dev, 0, H))
    spans = ((0, low // 2), (low, (levels - low) // 2))
    mine = [pl.ds(lo + half * n, n) for lo, n in spans]

    def wind_sends(part):
        out = []
        for s, q, src, dst in sides:
            for a, w in enumerate(winds):
                skip = 1 if s == 0 and a > 1 else 0
                size = H if s == 0 and a < 2 else H - 1
                out.append(
                    pltpu.make_async_remote_copy(
                        w.at[mine[part], src + skip : src + skip + size, :],
                        whalo.at[a, mine[part], dst + skip : dst + skip + size, :],
                        ws_sem.at[part, s, a], wr_sem.at[part, s, a],
                        device_id={"dom": q}, device_id_type=MESH,
                    )
                )
        for c in out:
            c.start()
        return out

    def state_sends(at, tag, lev):
        out = []
        for s, q, src, dst in sides:
            out.append(
                pltpu.make_async_remote_copy(
                    x_ref.at[tag, lev, src : src + H, :],
                    halo.at[tag, lev, dst : dst + H, :],
                    xs_sem.at[at, s], xr_sem.at[at, s],
                    device_id={"dom": q}, device_id_type=MESH,
                )
            )
        for c in out:
            c.start()
        return out

    low_winds = wind_sends(0)
    tops = []
    for s, q, src, dst in sides:
        c = pltpu.make_async_remote_copy(
            top_ref.at[src : src + H, :], thalo.at[dst : dst + H, :],
            ts_sem.at[s], tr_sem.at[s],
            device_id={"dom": q}, device_id_type=MESH,
        )
        c.start()
        tops.append(c)
    low_state = state_sends(0, slice(0, tags), slice(0, low))
    high_winds = wind_sends(1)
    high_state = [
        state_sends(1 + p, slice(2 * p, 2 * p + 2), slice(low, levels)) for p in range(tags // 2)
    ]

    def share_part(part):
        return pltpu.make_async_remote_copy(
            whalo.at[:, mine[part]], whalo.at[:, mine[part]], fs_sem.at[part], fr_sem.at[part],
            device_id={"grp": twin}, device_id_type=MESH,
        )

    def advance(left, cen, right, c):
        lv = pl.ds(0, cen.shape[1])
        north = pltpu.roll(cen, lats - 1, 2)
        south = pltpu.roll(cen, 1, 2)
        h = (
            coef[C0, c, lv][None] * cen
            + coef[CE, c, lv][None] * right
            + coef[CW, c, lv][None] * left
            + coef[CN, c, lv][None] * north
            + coef[CS, c, lv][None] * south
        )
        above = pltpu.roll(h, cen.shape[1] - 1, 1)
        return h + coef[UP, c, lv][None] * (above - h)

    blank = jnp.zeros((tags, 8, lats), jnp.float32)
    for c in (H, H + cols - 1):
        acc[:, c] = blank
    for n in range(4 * H):
        edge_acc[:, n] = blank


    @pl.loop(0, tags // 2)
    def _(p):
        ks = pl.ds(2 * p, 2)

        def run(c, carry, n, first):
            old = list(carry) + [state[ks, c + 1 + j] for j in range(n)]
            for j in range(n):
                new = advance(old[j], old[j + 1], old[j + 2], c + j)
                state[ks, c + j] = new
                if first:
                    acc[ks, c + j] = new[:, 0:8]
                else:
                    acc[ks, c + j] += new[:, 0:8]
            return old[n], old[n + 1]

        for t in range(1, ITERS + 1):
            start, size = H + t, cols - 2 * t
            carry = state[ks, start - 1], state[ks, start]
            save_l[ks, t - 1] = carry[1]
            if size % 4:
                carry = run(start, carry, size % 4, t == 1)
                start += size % 4
            carry = lax.fori_loop(
                0, size // 4, lambda b, v: run(start + 4 * b, v, 4, t == 1), carry
            )
            save_r[ks, t - 1] = carry[0]

    tag0 = grp * tags
    row = lax.broadcasted_iota(jnp.int32, (8, lats), 0)

    def chosen(here, lump):
        total = jnp.zeros((8, lats), jnp.float32)
        for k in range(tags):
            total += jnp.where(here == tag0 + k, turned(lump[k])[0], 0.0)
        return total

    @pl.loop(0, cols // 8)
    def _(i):
        here = regs[pl.ds(pl.multiple_of(8 * i, 8), 8), :]
        part1[pl.ds(pl.multiple_of(8 * i, 8), 8), :] = chosen(
            here, [acc[k, pl.ds(H + 8 * i, 8)] for k in range(tags)]
        )

    def to_peers(part, got, sems, peers):
        out = []
        for n, q in enumerate(peers):
            c = pltpu.make_async_remote_copy(
                part, got.at[n], sems.at[0, n], sems.at[1, n],
                device_id={"grp": q}, device_id_type=MESH,
            )
            c.start()
            out.append(c)
        return out

    def gathered(part, got, copies):
        for c in copies:
            c.wait_recv()
        value = part[...]
        for n in range(len(copies)):
            value += got[n]
        return value

    early_near = to_peers(part1, near1, n1_sem, near)

    def edge_coefs(lv, size):
        pad = levels // 2 * (size < levels)

        def part(a):
            if not pad:
                return whalo[a]
            return jnp.concatenate(
                [whalo[a, 0:size], jnp.zeros((pad - size, 2 * H, lats), jnp.float32)], axis=0
            )

        made, prime = derive(
            *[part(a) for a in range(5)], thalo[...], jnp.zeros((lv.size, lats), jnp.float32)
        )
        for m in range(6):
            coef[m, 0:H, lv] = made[m][0:H]
            coef[m, H + cols : 2 * H + cols, lv] = made[m][H:]
        first = prime[H - 1]
        coef[CW, H, lv] = first
        coef[C0, H, lv] = keep_first[lv] - first
        last = west_end[lv]
        coef[CW, H + cols, lv] = last
        coef[C0, H + cols, lv] = made[C0][H] + made[CW][H] - last

    def edges(store, ks, lv, shift, count_in):
        @pl.loop(1, ITERS + 1)
        def _(t):
            for base, at in ((t, t), (H + cols - t, H + cols - t - shift)):
                if base is t:
                    old = [store[ks, at - 1 + n] for n in range(H + 1)]
                    old.append(save_l[ks, t - 1, lv])
                else:
                    old = [save_r[ks, t - 1, lv]]
                    old += [store[ks, at + n] for n in range(H + 1)]
                for n in range(H):
                    new = advance(old[n], old[n + 1], old[n + 2], base + n)
                    store[ks, at + n] = new
                    if count_in:
                        edge_acc[ks, at + n] += new

    for c in low_winds:
        c.wait_recv()
    share0 = share_part(0)
    share0.start()
    for c in tops + low_state:
        c.wait_recv()
    share0.wait_recv()
    edge_coefs(pl.ds(0, 8), low)

    @pl.loop(0, tags // 2)
    def _(p):
        for j in range(2):
            k = 2 * p + j
            ring = turned(
                jnp.concatenate(
                    [halo[k, 0:low], jnp.zeros((8 - low, 2 * H, lats), jnp.float32)], axis=0
                )
            )
            surf[k, 0:H] = ring[0:H]
            surf[k, 3 * H : 4 * H] = ring[H:]
            surf[k, H : 2 * H] = state[k, H : 2 * H, 0:8]
            surf[k, 2 * H : 3 * H] = state[k, cols : cols + H, 0:8]
        edges(surf, pl.ds(2 * p, 2), pl.ds(0, 8), cols - 2 * H, True)

    here = jnp.where(row < H, regs[0:8, :], regs[cols - 8 : cols, :])
    part2[...] = chosen(here, [edge_acc[k, H : 3 * H] for k in range(tags)])

    late_near = to_peers(part2, near2, n2_sem, near)

    @pl.loop(0, tags)
    def _(k):
        @pl.loop(1, cols // 8 - 1)
        def _(i):
            at = pl.ds(pl.multiple_of(8 * i, 8), 8)
            lam_ref[k, :, at, :] = turned(state[k, pl.ds(H + 8 * i, 8)])

    mid1[...] = gathered(part1, near1, early_near)
    early_far = to_peers(mid1, far1, f1_sem, far)
    for c in high_winds:
        c.wait_recv()
    share1 = share_part(1)
    share1.start()
    mid2[...] = gathered(part2, near2, late_near)
    late_far = to_peers(mid2, far2, f2_sem, far)
    share1.wait_recv()
    edge_coefs(pl.ds(0, levels), levels)

    for p in range(tags // 2):
        for c in high_state[p]:
            c.wait_recv()
        for k in (2 * p, 2 * p + 1):
            ring = turned(halo[k])
            state[k, 0:H] = ring[0:H]
            state[k, H + cols : 2 * H + cols] = ring[H:]
        edges(state, pl.ds(2 * p, 2), pl.ds(0, levels), 0, False)
        for k in (2 * p, 2 * p + 1):
            for i in (0, cols // 8 - 1):
                lam_ref[k, :, 8 * i : 8 * i + 8, :] = turned(state[k, H + 8 * i : H + 8 * i + 8])

    grad_ref[...] = gathered(mid1, far1, early_far)
    ends = gathered(mid2, far2, late_far)
    grad_ref[0:8, :] += jnp.where(row < H, ends, 0.0)
    grad_ref[cols - 8 : cols, :] += jnp.where(row >= H, ends, 0.0)

    sent = low_winds + tops + low_state + high_winds + high_state[0] + high_state[1]
    for c in sent + [share0, share1] + early_near + early_far + late_near + late_far:
        c.wait_send()


def write_out(lam_ref, grad_ref, lam_out, grad_out, sem):
    copies = [
        pltpu.make_async_copy(lam_ref, lam_out, sem.at[0]),
        pltpu.make_async_copy(grad_ref, grad_out, sem.at[1]),
    ]
    for c in copies:
        c.start()
    for c in copies:
        c.wait()


def local(
    adjoint_state, east_wind, north_wind, east_diff, north_diff, mass_flux, region_map, cloud_top
):
    tags, levels, cols, lats = adjoint_state.shape
    groups = lax.axis_size("grp")
    f32 = jnp.float32
    wide = cols + 2 * ITERS
    dma = pltpu.SemaphoreType.DMA
    scratch = [
        pltpu.VMEM((tags, levels, cols, lats), f32),
        pltpu.VMEM((5, levels, cols, lats), f32),
        pltpu.VMEM((tags, wide, levels, lats), f32),
        pltpu.VMEM((6, wide, levels, lats), f32),
        pltpu.VMEM((cols, lats), jnp.int32),
        pltpu.VMEM((cols, lats), jnp.int32),
        pltpu.VMEM((tags, levels, 2 * ITERS, lats), f32),
        pltpu.VMEM((5, levels, 2 * ITERS, lats), f32),
        pltpu.VMEM((2 * ITERS, lats), jnp.int32),
        pltpu.VMEM((tags, ITERS, levels, lats), f32),
        pltpu.VMEM((tags, ITERS, levels, lats), f32),
        pltpu.VMEM((levels, lats), f32),
        pltpu.VMEM((tags, wide, 8, lats), f32),
        pltpu.VMEM((tags, 4 * ITERS, 8, lats), f32),
        pltpu.VMEM((cols, lats), f32),
        pltpu.VMEM((2 * ITERS, lats), f32),
        pltpu.VMEM((3, cols, lats), f32),
        pltpu.VMEM((3, 2 * ITERS, lats), f32),
        pltpu.VMEM((cols, lats), f32),
        pltpu.VMEM((2 * ITERS, lats), f32),
        pltpu.VMEM((groups // 4 - 1, cols, lats), f32),
        pltpu.VMEM((groups // 4 - 1, 2 * ITERS, lats), f32),
        pltpu.VMEM((tags, 4 * ITERS, 8, lats), f32),
        pltpu.VMEM((levels, lats), f32),
        dma((8,)),
        dma((1 + tags // 2, 2)),
        dma((1 + tags // 2, 2)),
        dma((2, 2, 5)),
        dma((2, 2, 5)),
        dma((2,)),
        dma((2,)),
        dma((2,)),
        dma((2,)),
        dma((2, 3)),
        dma((2, 3)),
        dma((2, groups // 4 - 1)),
        dma((2, groups // 4 - 1)),
    ]
    made = pl.pallas_call(
        kernel,
        name="adjoint_transport",
        out_shape=(
            pltpu.VMEM((tags, levels, cols, lats), f32),
            pltpu.VMEM((cols, lats), f32),
        ),
        in_specs=[pl.BlockSpec(memory_space=pltpu.HBM)] * 8,
        out_specs=(
            pl.BlockSpec(memory_space=pltpu.VMEM),
            pl.BlockSpec(memory_space=pltpu.VMEM),
        ),
        scratch_shapes=scratch,
        compiler_params=pltpu.CompilerParams(
            collective_id=0, has_side_effects=True, vmem_limit_bytes=58 << 20
        ),
    )(
        adjoint_state, east_wind, north_wind, east_diff, north_diff, mass_flux, region_map,
        cloud_top,
    )
    return pl.pallas_call(
        write_out,
        name="write_out",
        out_shape=tuple(jax.ShapeDtypeStruct(v.shape, v.dtype) for v in made),
        in_specs=[pl.BlockSpec(memory_space=pltpu.VMEM)] * 2,
        out_specs=(pl.BlockSpec(memory_space=pltpu.HBM),) * 2,
        scratch_shapes=[dma((2,))],
    )(*[pltpu.with_memory_space_constraint(v, pltpu.VMEM) for v in made])


def solution(mesh):
    return jax.shard_map(
        local,
        mesh=mesh,
        in_specs=(
            P("grp", None, "dom", None),
            P(None, "dom", None),
            P(None, "dom", None),
            P(None, "dom", None),
            P(None, "dom", None),
            P(None, "dom", None),
            P("dom", None),
            P("dom", None),
        ),
        out_specs=(P("grp", None, "dom", None), P("dom", None)),
        check_vma=False,
    )
```

```python
import jax
import jax.numpy as jnp
from jax import lax
from jax.experimental import pallas as pl
from jax.experimental.pallas import tpu as pltpu
from jax.sharding import PartitionSpec as P

ITERS = 4
MESH = pl.DeviceIdType.MESH
CE, CW, CN, CS, C0, UP = range(6)


def turned(value):
    return jnp.swapaxes(value, 0, 1)


def kernel(
    x_ref, ew_ref, nw_ref, ed_ref, nd_ref, mf_ref, reg_ref, top_ref,
    lam_ref, grad_ref,
    raw, wraw, state, coef, ctop, regs, halo, whalo, thalo, save_l, save_r, west_end,
    acc, edge_acc, part1, part2, near1, near2, mid1, mid2, far1, far2, surf, keep_first,
    in_sem, xs_sem, xr_sem, ws_sem, wr_sem, ts_sem, tr_sem, fs_sem, fr_sem, n1_sem, n2_sem, f1_sem, f2_sem,
):
    tags, levels, cols, lats = x_ref.shape
    groups = lax.axis_size("grp")
    count = lax.axis_size("dom")
    me = lax.axis_index("dom")
    grp = lax.axis_index("grp")
    east_dev = lax.rem(me + 1, count)
    west_dev = lax.rem(me + count - 1, count)
    half = lax.rem(grp, 2)
    twin = grp + 1 - 2 * half
    lane4 = lax.rem(grp, 4)
    near = [grp - lane4 + lax.rem(lane4 + d, 4) for d in range(1, 4)]
    far = [lax.rem(grp + 4 * d, groups) for d in range(1, groups // 4)]
    H = ITERS
    low = ITERS + 2

    winds = (ew_ref, ed_ref, nw_ref, nd_ref, mf_ref)
    barrier = pltpu.get_barrier_semaphore()
    for q in (east_dev, west_dev):
        pl.semaphore_signal(barrier, inc=1, device_id={"dom": q}, device_id_type=MESH)
    for q in near + far:
        pl.semaphore_signal(barrier, inc=1, device_id={"grp": q}, device_id_type=MESH)
    loads = [pltpu.make_async_copy(w, wraw.at[a], in_sem.at[a]) for a, w in enumerate(winds)]
    loads.append(pltpu.make_async_copy(top_ref, ctop, in_sem.at[5]))
    loads.append(pltpu.make_async_copy(reg_ref, regs, in_sem.at[6]))
    loads.append(pltpu.make_async_copy(x_ref, raw, in_sem.at[7]))
    for c in loads:
        c.start()

    def derive(ew, ed, nw, nd, mf, top, before):
        level = lax.broadcasted_iota(jnp.int32, ew.shape, 0)
        lane = lax.broadcasted_iota(jnp.int32, (8, ew.shape[0], lats), 2)
        lift = mf * (level < jnp.minimum(top, levels - 1)[None]).astype(jnp.float32)
        ew, ed, nw, nd, lift = turned(ew), turned(ed), turned(nw), turned(nd), turned(lift)
        east = jnp.maximum(ew, 0.0) + ed
        prime = jnp.maximum(-ew, 0.0) + ed
        west = jnp.concatenate([before[None], prime[:-1]], axis=0)
        north = jnp.where(lane < lats - 1, jnp.maximum(nw, 0.0) + nd, 0.0)
        south = jnp.where(lane > 0, pltpu.roll(jnp.maximum(-nw, 0.0) + nd, 1, 2), 0.0)
        keep = 1.0 - east - west - north - south
        return (east, west, north, south, keep, lift), prime

    for c in loads[:6]:
        c.wait()

    def derive_tile(i, before):
        at = pl.ds(pl.multiple_of(8 * i, 8), 8)
        made, prime = derive(*[wraw[a, :, at, :] for a in range(5)], ctop[at, :], before)
        for m in range(6):
            coef[m, pl.ds(H + 8 * i, 8)] = made[m]
        return prime[7]

    west_end[...] = lax.fori_loop(
        0, cols // 8, derive_tile, jnp.zeros((levels, lats), jnp.float32)
    )

    keep_first[...] = coef[C0, H]
    loads[7].wait()
    loads[6].wait()

    @pl.loop(0, tags)
    def _(k):
        @pl.loop(0, cols // 8)
        def _(i):
            at = pl.multiple_of(8 * i, 8)
            state[k, pl.ds(H + 8 * i, 8)] = turned(raw[k, :, pl.ds(at, 8), :])

    pl.semaphore_wait(barrier, 2 + len(near) + len(far))

    sides = ((0, east_dev, cols - H, 0), (1, west_dev, 0, H))
    spans = ((0, low // 2), (low, (levels - low) // 2))
    mine = [pl.ds(lo + half * n, n) for lo, n in spans]

    def wind_sends(part):
        out = []
        for s, q, src, dst in sides:
            for a, w in enumerate(winds):
                skip = 1 if s == 0 and a > 1 else 0
                size = H if s == 0 and a < 2 else H - 1
                out.append(
                    pltpu.make_async_remote_copy(
                        w.at[mine[part], src + skip : src + skip + size, :],
                        whalo.at[a, mine[part], dst + skip : dst + skip + size, :],
                        ws_sem.at[part, s, a], wr_sem.at[part, s, a],
                        device_id={"dom": q}, device_id_type=MESH,
                    )
                )
        for c in out:
            c.start()
        return out

    def state_sends(at, tag, lev):
        out = []
        for s, q, src, dst in sides:
            out.append(
                pltpu.make_async_remote_copy(
                    x_ref.at[tag, lev, src : src + H, :],
                    halo.at[tag, lev, dst : dst + H, :],
                    xs_sem.at[at, s], xr_sem.at[at, s],
                    device_id={"dom": q}, device_id_type=MESH,
                )
            )
        for c in out:
            c.start()
        return out

    low_winds = wind_sends(0)
    tops = []
    for s, q, src, dst in sides:
        c = pltpu.make_async_remote_copy(
            top_ref.at[src : src + H, :], thalo.at[dst : dst + H, :],
            ts_sem.at[s], tr_sem.at[s],
            device_id={"dom": q}, device_id_type=MESH,
        )
        c.start()
        tops.append(c)
    low_state = state_sends(0, slice(0, tags), slice(0, low))
    high_winds = wind_sends(1)
    high_state = [
        state_sends(1 + p, slice(2 * p, 2 * p + 2), slice(low, levels)) for p in range(tags // 2)
    ]

    def share_part(part):
        return pltpu.make_async_remote_copy(
            whalo.at[:, mine[part]], whalo.at[:, mine[part]], fs_sem.at[part], fr_sem.at[part],
            device_id={"grp": twin}, device_id_type=MESH,
        )

    def advance(left, cen, right, c):
        lv = pl.ds(0, cen.shape[1])
        north = pltpu.roll(cen, lats - 1, 2)
        south = pltpu.roll(cen, 1, 2)
        h = (
            coef[C0, c, lv][None] * cen
            + coef[CE, c, lv][None] * right
            + coef[CW, c, lv][None] * left
            + coef[CN, c, lv][None] * north
            + coef[CS, c, lv][None] * south
        )
        above = pltpu.roll(h, cen.shape[1] - 1, 1)
        return h + coef[UP, c, lv][None] * (above - h)

    blank = jnp.zeros((tags, 8, lats), jnp.float32)
    for c in (H, H + cols - 1):
        acc[:, c] = blank
    for n in range(4 * H):
        edge_acc[:, n] = blank


    @pl.loop(0, tags // 2)
    def _(p):
        ks = pl.ds(2 * p, 2)

        def run(c, carry, n, first):
            old = list(carry) + [state[ks, c + 1 + j] for j in range(n)]
            for j in range(n):
                new = advance(old[j], old[j + 1], old[j + 2], c + j)
                state[ks, c + j] = new
                if first:
                    acc[ks, c + j] = new[:, 0:8]
                else:
                    acc[ks, c + j] += new[:, 0:8]
            return old[n], old[n + 1]

        for t in range(1, ITERS + 1):
            start, size = H + t, cols - 2 * t
            carry = state[ks, start - 1], state[ks, start]
            save_l[ks, t - 1] = carry[1]
            if size % 8:
                carry = run(start, carry, size % 8, t == 1)
                start += size % 8
            carry = lax.fori_loop(
                0, size // 8, lambda b, v: run(start + 8 * b, v, 8, t == 1), carry
            )
            save_r[ks, t - 1] = carry[0]

    tag0 = grp * tags
    row = lax.broadcasted_iota(jnp.int32, (8, lats), 0)

    def chosen(here, lump):
        total = jnp.zeros((8, lats), jnp.float32)
        for k in range(tags):
            total += jnp.where(here == tag0 + k, turned(lump[k])[0], 0.0)
        return total

    @pl.loop(0, cols // 8)
    def _(i):
        here = regs[pl.ds(pl.multiple_of(8 * i, 8), 8), :]
        part1[pl.ds(pl.multiple_of(8 * i, 8), 8), :] = chosen(
            here, [acc[k, pl.ds(H + 8 * i, 8)] for k in range(tags)]
        )

    def to_peers(part, got, sems, peers):
        out = []
        for n, q in enumerate(peers):
            c = pltpu.make_async_remote_copy(
                part, got.at[n], sems.at[0, n], sems.at[1, n],
                device_id={"grp": q}, device_id_type=MESH,
            )
            c.start()
            out.append(c)
        return out

    def gathered(part, got, copies):
        for c in copies:
            c.wait_recv()
        value = part[...]
        for n in range(len(copies)):
            value += got[n]
        return value

    early_near = to_peers(part1, near1, n1_sem, near)

    def edge_coefs(lv, size):
        pad = levels // 2 * (size < levels)

        def part(a):
            if not pad:
                return whalo[a]
            return jnp.concatenate(
                [whalo[a, 0:size], jnp.zeros((pad - size, 2 * H, lats), jnp.float32)], axis=0
            )

        made, prime = derive(
            *[part(a) for a in range(5)], thalo[...], jnp.zeros((lv.size, lats), jnp.float32)
        )
        for m in range(6):
            coef[m, 0:H, lv] = made[m][0:H]
            coef[m, H + cols : 2 * H + cols, lv] = made[m][H:]
        first = prime[H - 1]
        coef[CW, H, lv] = first
        coef[C0, H, lv] = keep_first[lv] - first
        last = west_end[lv]
        coef[CW, H + cols, lv] = last
        coef[C0, H + cols, lv] = made[C0][H] + made[CW][H] - last

    def edges(store, ks, lv, shift, count_in):
        @pl.loop(1, ITERS + 1)
        def _(t):
            for base, at in ((t, t), (H + cols - t, H + cols - t - shift)):
                if base is t:
                    old = [store[ks, at - 1 + n] for n in range(H + 1)]
                    old.append(save_l[ks, t - 1, lv])
                else:
                    old = [save_r[ks, t - 1, lv]]
                    old += [store[ks, at + n] for n in range(H + 1)]
                for n in range(H):
                    new = advance(old[n], old[n + 1], old[n + 2], base + n)
                    store[ks, at + n] = new
                    if count_in:
                        edge_acc[ks, at + n] += new

    for c in low_winds:
        c.wait_recv()
    share0 = share_part(0)
    share0.start()
    for c in tops + low_state:
        c.wait_recv()
    share0.wait_recv()
    edge_coefs(pl.ds(0, 8), low)

    @pl.loop(0, tags // 2)
    def _(p):
        for j in range(2):
            k = 2 * p + j
            ring = turned(
                jnp.concatenate(
                    [halo[k, 0:low], jnp.zeros((8 - low, 2 * H, lats), jnp.float32)], axis=0
                )
            )
            surf[k, 0:H] = ring[0:H]
            surf[k, 3 * H : 4 * H] = ring[H:]
            surf[k, H : 2 * H] = state[k, H : 2 * H, 0:8]
            surf[k, 2 * H : 3 * H] = state[k, cols : cols + H, 0:8]
        edges(surf, pl.ds(2 * p, 2), pl.ds(0, 8), cols - 2 * H, True)

    here = jnp.where(row < H, regs[0:8, :], regs[cols - 8 : cols, :])
    part2[...] = chosen(here, [edge_acc[k, H : 3 * H] for k in range(tags)])

    late_near = to_peers(part2, near2, n2_sem, near)

    @pl.loop(0, tags)
    def _(k):
        @pl.loop(1, cols // 8 - 1)
        def _(i):
            at = pl.ds(pl.multiple_of(8 * i, 8), 8)
            lam_ref[k, :, at, :] = turned(state[k, pl.ds(H + 8 * i, 8)])

    for c in high_winds:
        c.wait_recv()
    share1 = share_part(1)
    share1.start()
    mid2[...] = gathered(part2, near2, late_near)
    late_far = to_peers(mid2, far2, f2_sem, far)
    mid1[...] = gathered(part1, near1, early_near)
    early_far = to_peers(mid1, far1, f1_sem, far)
    share1.wait_recv()
    edge_coefs(pl.ds(0, levels), levels)

    for p in range(tags // 2):
        for c in high_state[p]:
            c.wait_recv()
        for k in (2 * p, 2 * p + 1):
            ring = turned(halo[k])
            state[k, 0:H] = ring[0:H]
            state[k, H + cols : 2 * H + cols] = ring[H:]
        edges(state, pl.ds(2 * p, 2), pl.ds(0, levels), 0, False)
        for k in (2 * p, 2 * p + 1):
            for i in (0, cols // 8 - 1):
                lam_ref[k, :, 8 * i : 8 * i + 8, :] = turned(state[k, H + 8 * i : H + 8 * i + 8])

    grad_ref[...] = gathered(mid1, far1, early_far)
    ends = gathered(mid2, far2, late_far)
    grad_ref[0:8, :] += jnp.where(row < H, ends, 0.0)
    grad_ref[cols - 8 : cols, :] += jnp.where(row >= H, ends, 0.0)

    sent = low_winds + tops + low_state + high_winds + high_state[0] + high_state[1]
    for c in sent + [share0, share1] + early_near + early_far + late_near + late_far:
        c.wait_send()


def write_out(lam_ref, grad_ref, lam_out, grad_out, sem):
    copies = [
        pltpu.make_async_copy(lam_ref, lam_out, sem.at[0]),
        pltpu.make_async_copy(grad_ref, grad_out, sem.at[1]),
    ]
    for c in copies:
        c.start()
    for c in copies:
        c.wait()


def local(
    adjoint_state, east_wind, north_wind, east_diff, north_diff, mass_flux, region_map, cloud_top
):
    tags, levels, cols, lats = adjoint_state.shape
    groups = lax.axis_size("grp")
    f32 = jnp.float32
    wide = cols + 2 * ITERS
    dma = pltpu.SemaphoreType.DMA
    scratch = [
        pltpu.VMEM((tags, levels, cols, lats), f32),
        pltpu.VMEM((5, levels, cols, lats), f32),
        pltpu.VMEM((tags, wide, levels, lats), f32),
        pltpu.VMEM((6, wide, levels, lats), f32),
        pltpu.VMEM((cols, lats), jnp.int32),
        pltpu.VMEM((cols, lats), jnp.int32),
        pltpu.VMEM((tags, levels, 2 * ITERS, lats), f32),
        pltpu.VMEM((5, levels, 2 * ITERS, lats), f32),
        pltpu.VMEM((2 * ITERS, lats), jnp.int32),
        pltpu.VMEM((tags, ITERS, levels, lats), f32),
        pltpu.VMEM((tags, ITERS, levels, lats), f32),
        pltpu.VMEM((levels, lats), f32),
        pltpu.VMEM((tags, wide, 8, lats), f32),
        pltpu.VMEM((tags, 4 * ITERS, 8, lats), f32),
        pltpu.VMEM((cols, lats), f32),
        pltpu.VMEM((2 * ITERS, lats), f32),
        pltpu.VMEM((3, cols, lats), f32),
        pltpu.VMEM((3, 2 * ITERS, lats), f32),
        pltpu.VMEM((cols, lats), f32),
        pltpu.VMEM((2 * ITERS, lats), f32),
        pltpu.VMEM((groups // 4 - 1, cols, lats), f32),
        pltpu.VMEM((groups // 4 - 1, 2 * ITERS, lats), f32),
        pltpu.VMEM((tags, 4 * ITERS, 8, lats), f32),
        pltpu.VMEM((levels, lats), f32),
        dma((8,)),
        dma((1 + tags // 2, 2)),
        dma((1 + tags // 2, 2)),
        dma((2, 2, 5)),
        dma((2, 2, 5)),
        dma((2,)),
        dma((2,)),
        dma((2,)),
        dma((2,)),
        dma((2, 3)),
        dma((2, 3)),
        dma((2, groups // 4 - 1)),
        dma((2, groups // 4 - 1)),
    ]
    made = pl.pallas_call(
        kernel,
        name="adjoint_transport",
        out_shape=(
            pltpu.VMEM((tags, levels, cols, lats), f32),
            pltpu.VMEM((cols, lats), f32),
        ),
        in_specs=[pl.BlockSpec(memory_space=pltpu.HBM)] * 8,
        out_specs=(
            pl.BlockSpec(memory_space=pltpu.VMEM),
            pl.BlockSpec(memory_space=pltpu.VMEM),
        ),
        scratch_shapes=scratch,
        compiler_params=pltpu.CompilerParams(
            collective_id=0, has_side_effects=True, vmem_limit_bytes=58 << 20
        ),
    )(
        adjoint_state, east_wind, north_wind, east_diff, north_diff, mass_flux, region_map,
        cloud_top,
    )
    return pl.pallas_call(
        write_out,
        name="write_out",
        out_shape=tuple(jax.ShapeDtypeStruct(v.shape, v.dtype) for v in made),
        in_specs=[pl.BlockSpec(memory_space=pltpu.VMEM)] * 2,
        out_specs=(pl.BlockSpec(memory_space=pltpu.HBM),) * 2,
        scratch_shapes=[dma((2,))],
    )(*[pltpu.with_memory_space_constraint(v, pltpu.VMEM) for v in made])


def solution(mesh):
    return jax.shard_map(
        local,
        mesh=mesh,
        in_specs=(
            P("grp", None, "dom", None),
            P(None, "dom", None),
            P(None, "dom", None),
            P(None, "dom", None),
            P(None, "dom", None),
            P(None, "dom", None),
            P("dom", None),
            P("dom", None),
        ),
        out_specs=(P("grp", None, "dom", None), P("dom", None)),
        check_vma=False,
    )
```

```python
import jax
import jax.numpy as jnp
from jax import lax
from jax.experimental import pallas as pl
from jax.experimental.pallas import tpu as pltpu
from jax.sharding import PartitionSpec as P

ITERS = 4
MESH = pl.DeviceIdType.MESH
CE, CW, CN, CS, C0, UP = range(6)


def turned(value):
    return jnp.swapaxes(value, 0, 1)


def kernel(
    x_ref, ew_ref, nw_ref, ed_ref, nd_ref, mf_ref, reg_ref, top_ref,
    lam_ref, grad_ref,
    raw, wraw, state, coef, ctop, regs, halo, whalo, thalo, save_l, save_r, west_end,
    acc, edge_acc, part1, part2, near1, near2, mid1, mid2, far1, far2, surf, keep_first,
    in_sem, xs_sem, xr_sem, ws_sem, wr_sem, ts_sem, tr_sem, fs_sem, fr_sem, n1_sem, n2_sem, f1_sem, f2_sem,
):
    tags, levels, cols, lats = x_ref.shape
    groups = lax.axis_size("grp")
    count = lax.axis_size("dom")
    me = lax.axis_index("dom")
    grp = lax.axis_index("grp")
    east_dev = lax.rem(me + 1, count)
    west_dev = lax.rem(me + count - 1, count)
    half = lax.rem(grp, 2)
    twin = grp + 1 - 2 * half
    lane4 = lax.rem(grp, 4)
    near = [grp - lane4 + lax.rem(lane4 + d, 4) for d in range(1, 4)]
    far = [lax.rem(grp + 4 * d, groups) for d in range(1, groups // 4)]
    H = ITERS
    low = ITERS + 2

    winds = (ew_ref, ed_ref, nw_ref, nd_ref, mf_ref)
    barrier = pltpu.get_barrier_semaphore()
    for q in (east_dev, west_dev):
        pl.semaphore_signal(barrier, inc=1, device_id={"dom": q}, device_id_type=MESH)
    for q in near + far:
        pl.semaphore_signal(barrier, inc=1, device_id={"grp": q}, device_id_type=MESH)
    loads = [pltpu.make_async_copy(w, wraw.at[a], in_sem.at[a]) for a, w in enumerate(winds)]
    loads.append(pltpu.make_async_copy(top_ref, ctop, in_sem.at[5]))
    loads.append(pltpu.make_async_copy(reg_ref, regs, in_sem.at[6]))
    loads.append(pltpu.make_async_copy(x_ref, raw, in_sem.at[7]))
    for c in loads:
        c.start()

    def derive(ew, ed, nw, nd, mf, top, before):
        level = lax.broadcasted_iota(jnp.int32, ew.shape, 0)
        lane = lax.broadcasted_iota(jnp.int32, (8, ew.shape[0], lats), 2)
        lift = mf * (level < jnp.minimum(top, levels - 1)[None]).astype(jnp.float32)
        ew, ed, nw, nd, lift = turned(ew), turned(ed), turned(nw), turned(nd), turned(lift)
        east = jnp.maximum(ew, 0.0) + ed
        prime = jnp.maximum(-ew, 0.0) + ed
        west = jnp.concatenate([before[None], prime[:-1]], axis=0)
        north = jnp.where(lane < lats - 1, jnp.maximum(nw, 0.0) + nd, 0.0)
        south = jnp.where(lane > 0, pltpu.roll(jnp.maximum(-nw, 0.0) + nd, 1, 2), 0.0)
        keep = 1.0 - east - west - north - south
        return (east, west, north, south, keep, lift), prime

    for c in loads[:6]:
        c.wait()

    def derive_tile(i, before):
        at = pl.ds(pl.multiple_of(8 * i, 8), 8)
        made, prime = derive(*[wraw[a, :, at, :] for a in range(5)], ctop[at, :], before)
        for m in range(6):
            coef[m, pl.ds(H + 8 * i, 8)] = made[m]
        return prime[7]

    west_end[...] = lax.fori_loop(
        0, cols // 8, derive_tile, jnp.zeros((levels, lats), jnp.float32)
    )

    keep_first[...] = coef[C0, H]
    loads[7].wait()
    loads[6].wait()

    @pl.loop(0, tags)
    def _(k):
        @pl.loop(0, cols // 8)
        def _(i):
            at = pl.multiple_of(8 * i, 8)
            state[k, pl.ds(H + 8 * i, 8)] = turned(raw[k, :, pl.ds(at, 8), :])

    def advance(left, cen, right, c):
        lv = pl.ds(0, cen.shape[1])
        north = pltpu.roll(cen, lats - 1, 2)
        south = pltpu.roll(cen, 1, 2)
        h = (
            coef[C0, c, lv][None] * cen
            + coef[CE, c, lv][None] * right
            + coef[CW, c, lv][None] * left
            + coef[CN, c, lv][None] * north
            + coef[CS, c, lv][None] * south
        )
        above = pltpu.roll(h, cen.shape[1] - 1, 1)
        return h + coef[UP, c, lv][None] * (above - h)

    blank = jnp.zeros((tags, 8, lats), jnp.float32)
    for c in (H, H + cols - 1):
        acc[:, c] = blank
    for n in range(4 * H):
        edge_acc[:, n] = blank


    def interior(p):
        ks = pl.ds(2 * p, 2)

        def run(c, carry, n, first):
            old = list(carry) + [state[ks, c + 1 + j] for j in range(n)]
            for j in range(n):
                new = advance(old[j], old[j + 1], old[j + 2], c + j)
                state[ks, c + j] = new
                if first:
                    acc[ks, c + j] = new[:, 0:8]
                else:
                    acc[ks, c + j] += new[:, 0:8]
            return old[n], old[n + 1]

        for t in range(1, ITERS + 1):
            start, size = H + t, cols - 2 * t
            carry = state[ks, start - 1], state[ks, start]
            save_l[ks, t - 1] = carry[1]
            if size % 8:
                carry = run(start, carry, size % 8, t == 1)
                start += size % 8
            carry = lax.fori_loop(
                0, size // 8, lambda b, v: run(start + 8 * b, v, 8, t == 1), carry
            )
            save_r[ks, t - 1] = carry[0]

    ahead = jnp.where(lax.rem(me, count // 2) < 2, tags // 2, 0)

    @pl.loop(0, ahead)
    def _(p):
        interior(p)

    pl.semaphore_wait(barrier, 2 + len(near) + len(far))

    sides = ((0, east_dev, cols - H, 0), (1, west_dev, 0, H))
    spans = ((0, low // 2), (low, (levels - low) // 2))
    mine = [pl.ds(lo + half * n, n) for lo, n in spans]

    def wind_sends(part):
        out = []
        for s, q, src, dst in sides:
            for a, w in enumerate(winds):
                skip = 1 if s == 0 and a > 1 else 0
                size = H if s == 0 and a < 2 else H - 1
                out.append(
                    pltpu.make_async_remote_copy(
                        w.at[mine[part], src + skip : src + skip + size, :],
                        whalo.at[a, mine[part], dst + skip : dst + skip + size, :],
                        ws_sem.at[part, s, a], wr_sem.at[part, s, a],
                        device_id={"dom": q}, device_id_type=MESH,
                    )
                )
        for c in out:
            c.start()
        return out

    def state_sends(at, tag, lev):
        out = []
        for s, q, src, dst in sides:
            out.append(
                pltpu.make_async_remote_copy(
                    x_ref.at[tag, lev, src : src + H, :],
                    halo.at[tag, lev, dst : dst + H, :],
                    xs_sem.at[at, s], xr_sem.at[at, s],
                    device_id={"dom": q}, device_id_type=MESH,
                )
            )
        for c in out:
            c.start()
        return out

    low_winds = wind_sends(0)
    tops = []
    for s, q, src, dst in sides:
        c = pltpu.make_async_remote_copy(
            top_ref.at[src : src + H, :], thalo.at[dst : dst + H, :],
            ts_sem.at[s], tr_sem.at[s],
            device_id={"dom": q}, device_id_type=MESH,
        )
        c.start()
        tops.append(c)
    low_state = state_sends(0, slice(0, tags), slice(0, low - 1))
    high_winds = wind_sends(1)
    high_state = [
        state_sends(1 + p, slice(2 * p, 2 * p + 2), slice(low - 1, levels)) for p in range(tags // 2)
    ]

    def share_part(part):
        return pltpu.make_async_remote_copy(
            whalo.at[:, mine[part]], whalo.at[:, mine[part]], fs_sem.at[part], fr_sem.at[part],
            device_id={"grp": twin}, device_id_type=MESH,
        )

    @pl.loop(ahead, tags // 2)
    def _(p):
        interior(p)

    tag0 = grp * tags
    row = lax.broadcasted_iota(jnp.int32, (8, lats), 0)

    def chosen(here, lump):
        total = jnp.zeros((8, lats), jnp.float32)
        for k in range(tags):
            total += jnp.where(here == tag0 + k, turned(lump[k])[0], 0.0)
        return total

    @pl.loop(0, cols // 8)
    def _(i):
        here = regs[pl.ds(pl.multiple_of(8 * i, 8), 8), :]
        part1[pl.ds(pl.multiple_of(8 * i, 8), 8), :] = chosen(
            here, [acc[k, pl.ds(H + 8 * i, 8)] for k in range(tags)]
        )

    def to_peers(part, got, sems, peers):
        out = []
        for n, q in enumerate(peers):
            c = pltpu.make_async_remote_copy(
                part, got.at[n], sems.at[0, n], sems.at[1, n],
                device_id={"grp": q}, device_id_type=MESH,
            )
            c.start()
            out.append(c)
        return out

    def gathered(part, got, copies):
        for c in copies:
            c.wait_recv()
        value = part[...]
        for n in range(len(copies)):
            value += got[n]
        return value

    early_near = to_peers(part1, near1, n1_sem, near)

    def edge_coefs(lv, size):
        pad = levels // 2 * (size < levels)

        def part(a):
            if not pad:
                return whalo[a]
            return jnp.concatenate(
                [whalo[a, 0:size], jnp.zeros((pad - size, 2 * H, lats), jnp.float32)], axis=0
            )

        made, prime = derive(
            *[part(a) for a in range(5)], thalo[...], jnp.zeros((lv.size, lats), jnp.float32)
        )
        for m in range(6):
            coef[m, 0:H, lv] = made[m][0:H]
            coef[m, H + cols : 2 * H + cols, lv] = made[m][H:]
        first = prime[H - 1]
        coef[CW, H, lv] = first
        coef[C0, H, lv] = keep_first[lv] - first
        last = west_end[lv]
        coef[CW, H + cols, lv] = last
        coef[C0, H + cols, lv] = made[C0][H] + made[CW][H] - last

    def edges(store, ks, lv, shift, count_in):
        @pl.loop(1, ITERS + 1)
        def _(t):
            for base, at in ((t, t), (H + cols - t, H + cols - t - shift)):
                if base is t:
                    old = [store[ks, at - 1 + n] for n in range(H + 1)]
                    old.append(save_l[ks, t - 1, lv])
                else:
                    old = [save_r[ks, t - 1, lv]]
                    old += [store[ks, at + n] for n in range(H + 1)]
                for n in range(H):
                    new = advance(old[n], old[n + 1], old[n + 2], base + n)
                    store[ks, at + n] = new
                    if count_in:
                        edge_acc[ks, at + n] += new

    for c in low_winds:
        c.wait_recv()
    share0 = share_part(0)
    share0.start()
    for c in tops + low_state:
        c.wait_recv()
    share0.wait_recv()
    edge_coefs(pl.ds(0, 8), low)

    @pl.loop(0, tags // 2)
    def _(p):
        for j in range(2):
            k = 2 * p + j
            ring = turned(
                jnp.concatenate(
                    [halo[k, 0 : low - 1], jnp.zeros((9 - low, 2 * H, lats), jnp.float32)],
                    axis=0,
                )
            )
            surf[k, 0:H] = ring[0:H]
            surf[k, 3 * H : 4 * H] = ring[H:]
            surf[k, H : 2 * H] = state[k, H : 2 * H, 0:8]
            surf[k, 2 * H : 3 * H] = state[k, cols : cols + H, 0:8]
        edges(surf, pl.ds(2 * p, 2), pl.ds(0, 8), cols - 2 * H, True)

    here = jnp.where(row < H, regs[0:8, :], regs[cols - 8 : cols, :])
    part2[...] = chosen(here, [edge_acc[k, H : 3 * H] for k in range(tags)])

    late_near = to_peers(part2, near2, n2_sem, near)

    @pl.loop(0, tags)
    def _(k):
        @pl.loop(1, cols // 8 - 1)
        def _(i):
            at = pl.ds(pl.multiple_of(8 * i, 8), 8)
            lam_ref[k, :, at, :] = turned(state[k, pl.ds(H + 8 * i, 8)])

    for c in high_winds:
        c.wait_recv()
    share1 = share_part(1)
    share1.start()
    mid2[...] = gathered(part2, near2, late_near)
    late_far = to_peers(mid2, far2, f2_sem, far)
    mid1[...] = gathered(part1, near1, early_near)
    early_far = to_peers(mid1, far1, f1_sem, far)
    share1.wait_recv()
    edge_coefs(pl.ds(0, levels), levels)

    for p in range(tags // 2):
        for c in high_state[p]:
            c.wait_recv()
        for k in (2 * p, 2 * p + 1):
            ring = turned(halo[k])
            state[k, 0:H] = ring[0:H]
            state[k, H + cols : 2 * H + cols] = ring[H:]
        edges(state, pl.ds(2 * p, 2), pl.ds(0, levels), 0, False)
        for k in (2 * p, 2 * p + 1):
            for i in (0, cols // 8 - 1):
                lam_ref[k, :, 8 * i : 8 * i + 8, :] = turned(state[k, H + 8 * i : H + 8 * i + 8])

    grad_ref[...] = gathered(mid1, far1, early_far)
    ends = gathered(mid2, far2, late_far)
    grad_ref[0:8, :] += jnp.where(row < H, ends, 0.0)
    grad_ref[cols - 8 : cols, :] += jnp.where(row >= H, ends, 0.0)

    sent = low_winds + tops + low_state + high_winds + high_state[0] + high_state[1]
    for c in sent + [share0, share1] + early_near + early_far + late_near + late_far:
        c.wait_send()


def write_out(lam_ref, grad_ref, lam_out, grad_out, sem):
    copies = [
        pltpu.make_async_copy(lam_ref, lam_out, sem.at[0]),
        pltpu.make_async_copy(grad_ref, grad_out, sem.at[1]),
    ]
    for c in copies:
        c.start()
    for c in copies:
        c.wait()


def local(
    adjoint_state, east_wind, north_wind, east_diff, north_diff, mass_flux, region_map, cloud_top
):
    tags, levels, cols, lats = adjoint_state.shape
    groups = lax.axis_size("grp")
    f32 = jnp.float32
    wide = cols + 2 * ITERS
    dma = pltpu.SemaphoreType.DMA
    scratch = [
        pltpu.VMEM((tags, levels, cols, lats), f32),
        pltpu.VMEM((5, levels, cols, lats), f32),
        pltpu.VMEM((tags, wide, levels, lats), f32),
        pltpu.VMEM((6, wide, levels, lats), f32),
        pltpu.VMEM((cols, lats), jnp.int32),
        pltpu.VMEM((cols, lats), jnp.int32),
        pltpu.VMEM((tags, levels, 2 * ITERS, lats), f32),
        pltpu.VMEM((5, levels, 2 * ITERS, lats), f32),
        pltpu.VMEM((2 * ITERS, lats), jnp.int32),
        pltpu.VMEM((tags, ITERS, levels, lats), f32),
        pltpu.VMEM((tags, ITERS, levels, lats), f32),
        pltpu.VMEM((levels, lats), f32),
        pltpu.VMEM((tags, wide, 8, lats), f32),
        pltpu.VMEM((tags, 4 * ITERS, 8, lats), f32),
        pltpu.VMEM((cols, lats), f32),
        pltpu.VMEM((2 * ITERS, lats), f32),
        pltpu.VMEM((3, cols, lats), f32),
        pltpu.VMEM((3, 2 * ITERS, lats), f32),
        pltpu.VMEM((cols, lats), f32),
        pltpu.VMEM((2 * ITERS, lats), f32),
        pltpu.VMEM((groups // 4 - 1, cols, lats), f32),
        pltpu.VMEM((groups // 4 - 1, 2 * ITERS, lats), f32),
        pltpu.VMEM((tags, 4 * ITERS, 8, lats), f32),
        pltpu.VMEM((levels, lats), f32),
        dma((8,)),
        dma((1 + tags // 2, 2)),
        dma((1 + tags // 2, 2)),
        dma((2, 2, 5)),
        dma((2, 2, 5)),
        dma((2,)),
        dma((2,)),
        dma((2,)),
        dma((2,)),
        dma((2, 3)),
        dma((2, 3)),
        dma((2, groups // 4 - 1)),
        dma((2, groups // 4 - 1)),
    ]
    made = pl.pallas_call(
        kernel,
        name="adjoint_transport",
        out_shape=(
            pltpu.VMEM((tags, levels, cols, lats), f32),
            pltpu.VMEM((cols, lats), f32),
        ),
        in_specs=[pl.BlockSpec(memory_space=pltpu.HBM)] * 8,
        out_specs=(
            pl.BlockSpec(memory_space=pltpu.VMEM),
            pl.BlockSpec(memory_space=pltpu.VMEM),
        ),
        scratch_shapes=scratch,
        compiler_params=pltpu.CompilerParams(
            collective_id=0, has_side_effects=True, vmem_limit_bytes=58 << 20
        ),
    )(
        adjoint_state, east_wind, north_wind, east_diff, north_diff, mass_flux, region_map,
        cloud_top,
    )
    return pl.pallas_call(
        write_out,
        name="write_out",
        out_shape=tuple(jax.ShapeDtypeStruct(v.shape, v.dtype) for v in made),
        in_specs=[pl.BlockSpec(memory_space=pltpu.VMEM)] * 2,
        out_specs=(pl.BlockSpec(memory_space=pltpu.HBM),) * 2,
        scratch_shapes=[dma((2,))],
    )(*[pltpu.with_memory_space_constraint(v, pltpu.VMEM) for v in made])


def solution(mesh):
    return jax.shard_map(
        local,
        mesh=mesh,
        in_specs=(
            P("grp", None, "dom", None),
            P(None, "dom", None),
            P(None, "dom", None),
            P(None, "dom", None),
            P(None, "dom", None),
            P(None, "dom", None),
            P("dom", None),
            P("dom", None),
        ),
        out_specs=(P("grp", None, "dom", None), P("dom", None)),
        check_vma=False,
    )
```
